32 devices in a mesh: groups: 2 (over y), tm: 16 (over z, x, core), rows: 1.
Axes of the slice: x: 2, y: 2, z: 4, core: 2. Of those that a mesh axis runs over, the one named last changes fastest.
Arguments:
- frames: bfloat16 [64, 1, 160, 384], P(('groups', 'tm'), 'rows'), parts along dimension 0, may hold values from -6 to 6
- segment_ids: int32 [64], P('groups'), parts along dimension 0, may hold values from 0 to 3, never falling along the last dimension, each value on 1 to 16 neighbouring positions
- norm_gain: float32 [384], replicated, may hold values from 0.25 to 1.75
- conv_weight: bfloat16 [384, 3, 3, 3, 384], P('tm'), may hold values from -0.0625 to 0.0625
- attn_gain: float32 [384], replicated, may hold values from 0.25 to 1.75
- w_qkv: bfloat16 [384, 1152], replicated
- w_out: bfloat16 [384, 384], replicated, may hold values from -2.5 to 2.5
Outputs:
- summed: bfloat16 [64, 1, 160, 384], P(('groups', 'tm'), 'rows'), parts along dimension 0
- attended: bfloat16 [64, 1, 160, 384], P(('groups', 'tm'), 'rows'), parts along dimension 0
The draws below stay inside these ranges and needn't reach their ends.
There are 2 independent parts, one for each index of `groups`. The reference program is written for one: setup_inputs(seed, part) draws one part's arguments, and reference() takes and returns one part's arrays. A program takes and returns all parts, laid end to end along the dimension named above; an argument that names none is the same for every part. Nothing has to cross between parts.
Inputs may be any that keep to these rules, and one draw needn't show every extreme that they name: `segment_ids`: frames of one video are consecutive and ids never fall along the frames; every video has 1 to 16 frames and one has exactly 16.
All inputs are finite; a program needn't handle non-finite values.
Results may differ from the reference program's by a relative error of at most 0.013.
Values may be sent and summed in bfloat16 or wider, within the bound.
A program may use at most 64 MiB of HBM per device.

```python
import math
import jax
import jax.numpy as jnp
import numpy as np
from jax import lax

C = 384
W = 160
FRAMES = 32
ROWS = 1
SEGS = 4
MOST = 16


def draw_w_qkv(key, part):
    drawn = jax.random.normal(key, (C, 3 * C), jnp.float32) / math.sqrt(C)
    return drawn.astype(jnp.bfloat16)


def steps_of(own_key, shape, split, smallest, top_value):
    level, own = 1.0, jax.random.fold_in(own_key, 6)
    for axis_at, blocks in split:
        steps = jnp.exp(jax.random.uniform(jax.random.fold_in(own, axis_at), (blocks,), jnp.float32, smallest / len(split), top_value / len(split)))
        level = level * jnp.repeat(steps, shape[axis_at] // blocks).reshape([-1 if axis == axis_at else 1 for axis in range(len(shape))])
    return level


def split_up(amount, total, most, slope):
    portions = [(1 << 20) // math.isqrt(grade ** slope) + 1 for grade in range(2, amount + 1)]
    spare, holding = total - most - (amount - 1), [1] * (amount - 1)
    while spare > 0:
        candidates = [i for i in range(amount - 1) if holding[i] < most]
        pool, budget = sum([portions[i] for i in candidates]), spare
        for i in candidates:
            addition = min(most - holding[i], max(1, budget * portions[i] // pool), spare)
            holding[i] = holding[i] + addition
            spare = spare - addition
    return np.array([most] + holding)


def uneven(rng, number_of, total, reach, skew):
    if number_of == 2:
        one = jax.random.randint(rng, (), max(1, total - reach), min(reach, total - 1) + 1)
        return jnp.stack([one, total - one])
    tallies = jnp.asarray(split_up(number_of, total, reach, skew), jnp.int32)
    twos = (number_of - 1) // 2
    donor, receiver = tallies[1:1 + 2 * twos:2], tallies[2:2 + 2 * twos:2]
    margin = jnp.minimum(donor - 1, reach - receiver)
    shifted = jax.random.randint(jax.random.fold_in(rng, 1), (twos,), 0, 1 << 20) % (margin + 1)
    tallies = tallies.at[1:1 + 2 * twos:2].set(donor - shifted).at[2:2 + 2 * twos:2].set(receiver + shifted)
    return tallies[jax.random.permutation(jax.random.fold_in(rng, 2), number_of)]


def centred(key, shape, spread, most, shards=(), held_as=jnp.bfloat16):
    values = jax.random.normal(key, shape, jnp.float32) * spread
    if len(shards) > 0:
        values = steps_of(key, shape, shards, -0.22, 0.18) * values
    return jnp.clip(values, min=-most, max=most).astype(held_as)


def setup_inputs(seed: int = 0, part: int = 0) -> dict:
    key_of = jax.random.split(jax.random.key(seed), 8)
    part_splits = jax.random.split(jax.random.fold_in(key_of[7], part), 8)
    return {
        "frames": centred(part_splits[0], (FRAMES, ROWS, W, C), 1.0, 6.0, ((0, 16),)),
        "segment_ids": jnp.searchsorted(jnp.cumsum(uneven(part_splits[1], SEGS, FRAMES, MOST, 1)), jnp.arange(FRAMES), side="right").astype(jnp.int32),
        "norm_gain": jnp.clip(1.0 + 0.15 * jax.random.normal(key_of[2], (C,), jnp.float32), 0.25, 1.75),
        "conv_weight": centred(key_of[3], (C, 3, 3, 3, C), (27 * C) ** -0.5, 0.0625, ((0, 16),)),
        "attn_gain": jnp.clip(1.0 + 0.15 * jax.random.normal(key_of[4], (C,), jnp.float32), 0.25, 1.75),
        "w_qkv": draw_w_qkv(jax.random.fold_in(key_of[7], 71), part),
        "w_out": centred(key_of[6], (C, C), (max(C // 64, 1)) ** -0.5, 2.5),
    }


EPSILON = 1e-06

def normalize(values, gain):
    mean_square = lax.optimization_barrier(jnp.mean(values * values, axis=-1, keepdims=True))
    return values * lax.rsqrt(mean_square + EPSILON) * gain

def product(left, right):
    return jnp.dot(left.astype(jnp.float32), right.astype(jnp.float32), precision=lax.Precision.HIGHEST)

def attend_frame(operands):
    queries, keys, values = operands
    scores = product(queries, keys.T) * C ** (-0.5)
    top = lax.optimization_barrier(jnp.max(scores, axis=-1, keepdims=True))
    expo = jnp.exp(scores - top)
    weights = expo.astype(jnp.bfloat16)
    mixed = product(weights, values) / lax.optimization_barrier(jnp.sum(expo, axis=-1, keepdims=True))
    return mixed.astype(jnp.bfloat16)

def reference(frames, segment_ids, norm_gain, conv_weight, attn_gain, w_qkv, w_out):
    inputs = frames.astype(jnp.float32)
    activated = jax.nn.silu(normalize(inputs, norm_gain)).astype(jnp.bfloat16)
    padded = jnp.pad(activated, ((2, 0), (1, 1), (1, 1), (0, 0)))
    padded_ids = jnp.concatenate([jnp.full((2,), -1, jnp.int32), segment_ids.astype(jnp.int32)])
    convolved = jnp.zeros((FRAMES * ROWS * W, C), jnp.float32)
    for tap_t in range(3):
        valid = (padded_ids[tap_t:tap_t + FRAMES] == segment_ids).astype(jnp.bfloat16)
        for tap_h in range(3):
            for tap_w in range(3):
                window = padded[tap_t:tap_t + FRAMES, tap_h:tap_h + ROWS, tap_w:tap_w + W, :]
                window = window * valid[:, None, None, None]
                convolved = convolved + product(window.reshape(-1, C), conv_weight[:, tap_t, tap_h, tap_w, :])
    convolved = convolved.reshape(FRAMES, ROWS, W, C)
    summed = (inputs + convolved).astype(jnp.bfloat16)
    normed = normalize(summed.astype(jnp.float32), attn_gain).astype(jnp.bfloat16)
    projected = product(normed.reshape(-1, C), w_qkv).reshape(FRAMES, ROWS * W, 3 * C)
    queries = projected[:, :, :C].astype(jnp.bfloat16)
    keys = projected[:, :, C:2 * C].astype(jnp.bfloat16)
    values = projected[:, :, 2 * C:].astype(jnp.bfloat16)
    mixed = lax.map(attend_frame, (queries, keys, values))
    attended = product(mixed.reshape(-1, C), w_out).astype(jnp.bfloat16)
    return (summed, attended.reshape(FRAMES, ROWS, W, C))
```

```python
import jax
import jax.numpy as jnp
from jax import lax
from jax.sharding import Mesh
from jax.sharding import PartitionSpec as P

C = 384


EPSILON = 1e-06


def passed_along(value, axis, steps):
    count = lax.axis_size(axis)
    leading, last = (max(0, -steps), min(count, count - steps))
    return lax.ppermute(value, axis, [(source, source + steps) for source in range(leading, last)])


def with_halo(cells, sides, width):
    for axis, dim in sides:
        count = lax.axis_size(axis)
        ends = count - 1
        head = lax.slice_in_dim(cells, 0, width, axis=dim)
        tail = lax.slice_in_dim(cells, cells.shape[dim] - width, cells.shape[dim], axis=dim)
        cells = jnp.concatenate(
            [
                lax.ppermute(tail, axis, [(i, (i + 1) % count) for i in range(ends)]),
                cells,
                lax.ppermute(head, axis, [((i + 1) % count, i) for i in range(ends)]),
            ],
            axis=dim,
        )
    return cells


def normalize(values, gain):
    mean_square = jnp.mean(values * values, axis=-1, keepdims=True)
    return values * lax.rsqrt(mean_square + EPSILON) * gain


def absorb(carry, queries, keys, values):
    running_max, running_sum, running_acc = carry
    scores = jnp.einsum("fqc,fkc->fqk", queries, keys, preferred_element_type=jnp.float32) * C ** (
        -0.5
    )
    new_max = jnp.maximum(running_max, jnp.max(scores, axis=-1))
    expo = jnp.exp(scores - new_max[:, :, None])
    new_sum = jnp.sum(expo, axis=-1)
    update = jnp.einsum(
        "fqk,fkc->fqc", expo.astype(jnp.bfloat16), values, preferred_element_type=jnp.float32
    )
    return (new_max, new_sum, update)


def body(frames, segment_ids, norm_gain, conv_weight, attn_gain, w_qkv, w_out):
    depth, height, across, width = frames.shape
    chips = lax.axis_size("chip")
    core = lax.axis_index("core")
    inputs = frames.astype(jnp.float32)
    activated = jax.nn.silu(normalize(inputs, norm_gain)).astype(jnp.bfloat16)
    position = lax.axis_index("chip") * 2 + core
    first = position * depth
    padded_ids = jnp.concatenate([jnp.full((2,), -1, jnp.int32), segment_ids])
    local_ids = lax.dynamic_slice_in_dim(padded_ids, first, depth + 2)
    own_ids = local_ids[2:]
    earlier = lax.ppermute(
        activated, ("chip", "core"), [(source, source + 1) for source in range(2 * chips - 1)]
    )
    extended = with_halo(jnp.concatenate([earlier, activated], 0), (("rows", 1),), 1)
    extended = jnp.pad(extended, ((0, 0), (0, 0), (1, 1), (0, 0)))
    masked = jnp.stack(
        [
            extended[tap_t : tap_t + depth]
            * (local_ids[tap_t : tap_t + depth] == own_ids).astype(jnp.bfloat16)[
                :, None, None, None
            ]
            for tap_t in range(3)
        ]
    )
    share = width // (2 * chips)
    sets = masked.reshape(masked.shape[:-1] + (chips, 2, share))
    first_set = sets[..., 0, :].reshape(masked.shape[:-1] + (chips * share,))
    second_set = sets[..., 1, :].reshape(masked.shape[:-1] + (chips * share,))
    mine = jnp.where(core == 0, first_set, second_set)
    other = jnp.where(core == 0, second_set, first_set)
    swap = [(0, 1), (1, 0)]
    received = lax.ppermute(other, "core", swap)
    both = jnp.concatenate([mine, received], axis=1)
    total = jnp.zeros((2 * depth, height, across, width), jnp.float32)
    piece = lax.all_gather(conv_weight, "chip", axis=0, tiled=True)
    for tap_t in range(3):
        for tap_h in range(3):
            for tap_w in range(3):
                window = both[tap_t, :, tap_h : tap_h + height, tap_w : tap_w + across, :]
                total = total + jnp.einsum(
                    "fhwc,cd->fhwd",
                    window,
                    piece[:, tap_t, tap_h, tap_w, :],
                    preferred_element_type=jnp.float32,
                )
    returned = lax.ppermute(total[depth:], "core", swap)
    total = total[:depth] + returned
    summed = (inputs + total).astype(jnp.bfloat16)
    normed = normalize(summed.astype(jnp.float32), attn_gain).astype(jnp.bfloat16)
    flat = normed.reshape(depth, height * across, width)
    positions = height * across
    initial = (
        jnp.full((depth, positions), -1e30, jnp.float32),
        jnp.zeros((depth, positions), jnp.float32),
        jnp.zeros((depth, positions, width), jnp.float32),
    )
    projected = jnp.einsum("fpc,cd->fpd", flat, w_qkv, preferred_element_type=jnp.float32)
    queries = projected[:, :, :width].astype(jnp.bfloat16)
    keys = projected[:, :, width : 2 * width].astype(jnp.bfloat16)
    values = projected[:, :, 2 * width :].astype(jnp.bfloat16)
    result = absorb(
        initial,
        queries,
        lax.all_gather(keys, "rows", axis=1, tiled=True),
        lax.all_gather(values, "rows", axis=1, tiled=True),
    )
    mixed = (result[2] / result[1][:, :, None]).astype(jnp.bfloat16)
    attended = jnp.einsum("fpc,cd->fpd", mixed, w_out, preferred_element_type=jnp.float32).astype(
        jnp.bfloat16
    )
    return (summed, attended.reshape(depth, height, across, width))


def solution(mesh):
    groups, tm, rows = mesh.devices.shape
    split = Mesh(mesh.devices.reshape(groups, tm // 2, 2, rows), ("groups", "chip", "core", "rows"))
    return jax.shard_map(
        body,
        mesh=split,
        in_specs=(
            P(("groups", "chip", "core"), "rows", None, None),
            P("groups"),
            P(),
            P(("chip", "core"), None, None, None, None),
            P(),
            P(),
            P(),
        ),
        out_specs=(
            P(("groups", "chip", "core"), "rows", None, None),
            P(("groups", "chip", "core"), "rows", None, None),
        ),
        check_vma=False,
    )
```

```python
import jax
import jax.numpy as jnp
from jax import lax
from jax.sharding import Mesh
from jax.sharding import PartitionSpec as P

C = 384


EPSILON = 1e-06


def passed_along(value, axis, steps):
    count = lax.axis_size(axis)
    leading, last = (max(0, -steps), min(count, count - steps))
    return lax.ppermute(value, axis, [(source, source + steps) for source in range(leading, last)])


def with_halo(cells, sides, width):
    for axis, dim in sides:
        count = lax.axis_size(axis)
        ends = count - 1
        head = lax.slice_in_dim(cells, 0, width, axis=dim)
        tail = lax.slice_in_dim(cells, cells.shape[dim] - width, cells.shape[dim], axis=dim)
        cells = jnp.concatenate(
            [
                lax.ppermute(tail, axis, [(i, (i + 1) % count) for i in range(ends)]),
                cells,
                lax.ppermute(head, axis, [((i + 1) % count, i) for i in range(ends)]),
            ],
            axis=dim,
        )
    return cells


def normalize(values, gain):
    mean_square = jnp.mean(values * values, axis=-1, keepdims=True)
    return values * lax.rsqrt(mean_square + EPSILON) * gain


def absorb(carry, queries, keys, values):
    running_max, running_sum, running_acc = carry
    scores = jnp.einsum("fqc,fkc->fqk", queries, keys, preferred_element_type=jnp.float32) * C ** (
        -0.5
    )
    new_max = jnp.maximum(running_max, jnp.max(scores, axis=-1))
    expo = jnp.exp(scores - new_max[:, :, None])
    new_sum = jnp.sum(expo, axis=-1)
    update = jnp.einsum(
        "fqk,fkc->fqc", expo.astype(jnp.bfloat16), values, preferred_element_type=jnp.float32
    )
    return (new_max, new_sum, update)


def body(frames, segment_ids, norm_gain, conv_weight, attn_gain, w_qkv, w_out):
    depth, height, across, width = frames.shape
    chips = lax.axis_size("chip")
    core = lax.axis_index("core")
    inputs = frames.astype(jnp.float32)
    activated = jax.nn.silu(normalize(inputs, norm_gain)).astype(jnp.bfloat16)
    position = lax.axis_index("chip") * 2 + core
    first = position * depth
    padded_ids = jnp.concatenate([jnp.full((2,), -1, jnp.int32), segment_ids])
    local_ids = lax.dynamic_slice_in_dim(padded_ids, first, depth + 2)
    own_ids = local_ids[2:]
    earlier = lax.ppermute(
        activated, ("chip", "core"), [(source, source + 1) for source in range(2 * chips - 1)]
    )
    extended = with_halo(jnp.concatenate([earlier, activated], 0), (("rows", 1),), 1)
    extended = jnp.pad(extended, ((0, 0), (0, 0), (1, 1), (0, 0)))
    masked = jnp.stack(
        [
            extended[tap_t : tap_t + depth]
            * (local_ids[tap_t : tap_t + depth] == own_ids).astype(jnp.bfloat16)[
                :, None, None, None
            ]
            for tap_t in range(3)
        ]
    )
    swap = [(0, 1), (1, 0)]
    received = lax.ppermute(masked, "core", swap)
    both = jnp.concatenate([masked, received], axis=1)
    total = jnp.zeros((2 * depth, height, across, width), jnp.float32)
    gathered = lax.all_gather(conv_weight, "chip", axis=0)
    keep = (lax.broadcasted_iota(jnp.int32, (1, 2, 1, 1, 1, 1, 1), 1) == core).astype(jnp.bfloat16)
    piece = (gathered[:, None] * keep).reshape((width,) + conv_weight.shape[1:])
    for tap_t in range(3):
        for tap_h in range(3):
            for tap_w in range(3):
                window = both[tap_t, :, tap_h : tap_h + height, tap_w : tap_w + across, :]
                total = total + jnp.einsum(
                    "fhwc,cd->fhwd",
                    window,
                    piece[:, tap_t, tap_h, tap_w, :],
                    preferred_element_type=jnp.float32,
                )
    returned = lax.ppermute(total[depth:], "core", swap)
    total = total[:depth] + returned
    summed = (inputs + total).astype(jnp.bfloat16)
    normed = normalize(summed.astype(jnp.float32), attn_gain).astype(jnp.bfloat16)
    flat = normed.reshape(depth, height * across, width)
    positions = height * across
    initial = (
        jnp.full((depth, positions), -1e30, jnp.float32),
        jnp.zeros((depth, positions), jnp.float32),
        jnp.zeros((depth, positions, width), jnp.float32),
    )
    projected = jnp.einsum("fpc,cd->fpd", flat, w_qkv, preferred_element_type=jnp.float32)
    queries = projected[:, :, :width].astype(jnp.bfloat16)
    keys = projected[:, :, width : 2 * width].astype(jnp.bfloat16)
    values = projected[:, :, 2 * width :].astype(jnp.bfloat16)
    result = absorb(
        initial,
        queries,
        lax.all_gather(keys, "rows", axis=1, tiled=True),
        lax.all_gather(values, "rows", axis=1, tiled=True),
    )
    mixed = (result[2] / result[1][:, :, None]).astype(jnp.bfloat16)
    attended = jnp.einsum("fpc,cd->fpd", mixed, w_out, preferred_element_type=jnp.float32).astype(
        jnp.bfloat16
    )
    return (summed, attended.reshape(depth, height, across, width))


def solution(mesh):
    groups, tm, rows = mesh.devices.shape
    split = Mesh(mesh.devices.reshape(groups, tm // 2, 2, rows), ("groups", "chip", "core", "rows"))
    return jax.shard_map(
        body,
        mesh=split,
        in_specs=(
            P(("groups", "chip", "core"), "rows", None, None),
            P("groups"),
            P(),
            P(("chip", "core"), None, None, None, None),
            P(),
            P(),
            P(),
        ),
        out_specs=(
            P(("groups", "chip", "core"), "rows", None, None),
            P(("groups", "chip", "core"), "rows", None, None),
        ),
        check_vma=False,
    )
```

```python
import jax
import jax.numpy as jnp
from jax import lax
from jax.sharding import Mesh
from jax.sharding import PartitionSpec as P

C = 384


EPSILON = 1e-06


def passed_along(value, axis, steps):
    count = lax.axis_size(axis)
    leading, last = (max(0, -steps), min(count, count - steps))
    return lax.ppermute(value, axis, [(source, source + steps) for source in range(leading, last)])


def with_halo(cells, sides, width):
    for axis, dim in sides:
        count = lax.axis_size(axis)
        ends = count - 1
        head = lax.slice_in_dim(cells, 0, width, axis=dim)
        tail = lax.slice_in_dim(cells, cells.shape[dim] - width, cells.shape[dim], axis=dim)
        cells = jnp.concatenate(
            [
                lax.ppermute(tail, axis, [(i, (i + 1) % count) for i in range(ends)]),
                cells,
                lax.ppermute(head, axis, [((i + 1) % count, i) for i in range(ends)]),
            ],
            axis=dim,
        )
    return cells


def normalize(values, gain):
    mean_square = jnp.mean(values * values, axis=-1, keepdims=True)
    return values * lax.rsqrt(mean_square + EPSILON) * gain


def absorb(carry, queries, keys, values):
    running_max, running_sum, running_acc = carry
    scores = jnp.einsum("fqc,fkc->fqk", queries, keys, preferred_element_type=jnp.float32) * C ** (
        -0.5
    )
    new_max = jnp.maximum(running_max, jnp.max(scores, axis=-1))
    expo = jnp.exp(scores - new_max[:, :, None])
    new_sum = jnp.sum(expo, axis=-1)
    update = jnp.einsum(
        "fqk,fkc->fqc", expo.astype(jnp.bfloat16), values, preferred_element_type=jnp.float32
    )
    return (new_max, new_sum, update)


def body(frames, segment_ids, norm_gain, conv_weight, attn_gain, w_qkv, w_out):
    depth, height, across, width = frames.shape
    chips = lax.axis_size("chip")
    core = lax.axis_index("core")
    inputs = frames.astype(jnp.float32)
    activated = jax.nn.silu(normalize(inputs, norm_gain)).astype(jnp.bfloat16)
    position = lax.axis_index("chip") * 2 + core
    first = position * depth
    padded_ids = jnp.concatenate([jnp.full((2,), -1, jnp.int32), segment_ids])
    local_ids = lax.dynamic_slice_in_dim(padded_ids, first, depth + 2)
    own_ids = local_ids[2:]
    earlier = lax.ppermute(
        activated, ("chip", "core"), [(source, source + 1) for source in range(2 * chips - 1)]
    )
    extended = with_halo(jnp.concatenate([earlier, activated], 0), (("rows", 1),), 1)
    extended = jnp.pad(extended, ((0, 0), (0, 0), (1, 1), (0, 0)))
    masked = jnp.stack(
        [
            extended[tap_t : tap_t + depth]
            * (local_ids[tap_t : tap_t + depth] == own_ids).astype(jnp.bfloat16)[
                :, None, None, None
            ]
            for tap_t in range(3)
        ]
    )
    swap = [(0, 1), (1, 0)]
    received = lax.ppermute(masked, "core", swap)
    both = jnp.concatenate([masked, received], axis=1)
    total = jnp.zeros((2 * depth, height, across, width), jnp.float32)
    shifted = [conv_weight] + [
        lax.ppermute(conv_weight, "chip", [(i, (i + shift) % chips) for i in range(chips)])
        for shift in range(1, chips)
    ]
    order = (lax.axis_index("chip") - jnp.arange(chips)) % chips
    gathered = jnp.take(jnp.stack(shifted), order, axis=0)
    keep = (lax.broadcasted_iota(jnp.int32, (1, 2, 1, 1, 1, 1, 1), 1) == core).astype(jnp.bfloat16)
    piece = (gathered[:, None] * keep).reshape((width,) + conv_weight.shape[1:])
    for tap_t in range(3):
        for tap_h in range(3):
            for tap_w in range(3):
                window = both[tap_t, :, tap_h : tap_h + height, tap_w : tap_w + across, :]
                total = total + jnp.einsum(
                    "fhwc,cd->fhwd",
                    window,
                    piece[:, tap_t, tap_h, tap_w, :],
                    preferred_element_type=jnp.float32,
                )
    returned = lax.ppermute(total[depth:], "core", swap)
    total = total[:depth] + returned
    summed = (inputs + total).astype(jnp.bfloat16)
    normed = normalize(summed.astype(jnp.float32), attn_gain).astype(jnp.bfloat16)
    flat = normed.reshape(depth, height * across, width)
    positions = height * across
    initial = (
        jnp.full((depth, positions), -1e30, jnp.float32),
        jnp.zeros((depth, positions), jnp.float32),
        jnp.zeros((depth, positions, width), jnp.float32),
    )
    projected = jnp.einsum("fpc,cd->fpd", flat, w_qkv, preferred_element_type=jnp.float32)
    queries = projected[:, :, :width].astype(jnp.bfloat16)
    keys = projected[:, :, width : 2 * width].astype(jnp.bfloat16)
    values = projected[:, :, 2 * width :].astype(jnp.bfloat16)
    result = absorb(
        initial,
        queries,
        lax.all_gather(keys, "rows", axis=1, tiled=True),
        lax.all_gather(values, "rows", axis=1, tiled=True),
    )
    mixed = (result[2] / result[1][:, :, None]).astype(jnp.bfloat16)
    attended = jnp.einsum("fpc,cd->fpd", mixed, w_out, preferred_element_type=jnp.float32).astype(
        jnp.bfloat16
    )
    return (summed, attended.reshape(depth, height, across, width))


def solution(mesh):
    groups, tm, rows = mesh.devices.shape
    split = Mesh(mesh.devices.reshape(groups, tm // 2, 2, rows), ("groups", "chip", "core", "rows"))
    return jax.shard_map(
        body,
        mesh=split,
        in_specs=(
            P(("groups", "chip", "core"), "rows", None, None),
            P("groups"),
            P(),
            P(("chip", "core"), None, None, None, None),
            P(),
            P(),
            P(),
        ),
        out_specs=(
            P(("groups", "chip", "core"), "rows", None, None),
            P(("groups", "chip", "core"), "rows", None, None),
        ),
        check_vma=False,
    )
```

```python
import jax
import jax.numpy as jnp
from jax import lax
from jax.sharding import PartitionSpec as P

C = 384


EPSILON = 1e-06


def passed_along(value, axis, steps):
    count = lax.axis_size(axis)
    leading, last = (max(0, -steps), min(count, count - steps))
    return lax.ppermute(value, axis, [(source, source + steps) for source in range(leading, last)])


def with_halo(cells, sides, width):
    for axis, dim in sides:
        count = lax.axis_size(axis)
        ends = count - 1
        head = lax.slice_in_dim(cells, 0, width, axis=dim)
        tail = lax.slice_in_dim(cells, cells.shape[dim] - width, cells.shape[dim], axis=dim)
        cells = jnp.concatenate(
            [
                lax.ppermute(tail, axis, [(i, (i + 1) % count) for i in range(ends)]),
                cells,
                lax.ppermute(head, axis, [((i + 1) % count, i) for i in range(ends)]),
            ],
            axis=dim,
        )
    return cells


def normalize(values, gain):
    mean_square = jnp.mean(values * values, axis=-1, keepdims=True)
    return values * lax.rsqrt(mean_square + EPSILON) * gain


def absorb(carry, queries, keys, values):
    running_max, running_sum, running_acc = carry
    scores = jnp.einsum("fqc,fkc->fqk", queries, keys, preferred_element_type=jnp.float32) * C ** (
        -0.5
    )
    new_max = jnp.maximum(running_max, jnp.max(scores, axis=-1))
    expo = jnp.exp(scores - new_max[:, :, None])
    new_sum = jnp.sum(expo, axis=-1)
    update = jnp.einsum(
        "fqk,fkc->fqc", expo.astype(jnp.bfloat16), values, preferred_element_type=jnp.float32
    )
    return (new_max, new_sum, update)


def body(frames, segment_ids, norm_gain, conv_weight, attn_gain, w_qkv, w_out):
    depth, height, across, width = frames.shape
    inputs = frames.astype(jnp.float32)
    activated = jax.nn.silu(normalize(inputs, norm_gain)).astype(jnp.bfloat16)
    first = lax.axis_index("tm") * depth
    padded_ids = jnp.concatenate([jnp.full((2,), -1, jnp.int32), segment_ids])
    local_ids = lax.dynamic_slice_in_dim(padded_ids, first, depth + 2)
    own_ids = local_ids[2:]
    earlier = passed_along(activated, "tm", 1)
    extended = with_halo(jnp.concatenate([earlier, activated], 0), (("rows", 1),), 1)
    extended = jnp.pad(extended, ((0, 0), (0, 0), (1, 1), (0, 0)))
    masked = jnp.stack(
        [
            extended[tap_t : tap_t + depth]
            * (local_ids[tap_t : tap_t + depth] == own_ids).astype(jnp.bfloat16)[
                :, None, None, None
            ]
            for tap_t in range(3)
        ]
    )
    total = jnp.zeros((depth, height, across, width), jnp.float32)
    halves = conv_weight.reshape((2, conv_weight.shape[0] // 2) + conv_weight.shape[1:])
    half = lax.dynamic_index_in_dim(halves, lax.axis_index("groups"), 0, keepdims=False)
    gathered = lax.all_gather(half, ("groups", "tm"), axis=0)
    gathered = gathered.reshape((2, gathered.shape[0] // 2) + half.shape)
    piece = jnp.swapaxes(gathered, 0, 1).reshape((width,) + conv_weight.shape[1:])
    for tap_t in range(3):
        for tap_h in range(3):
            for tap_w in range(3):
                window = masked[tap_t, :, tap_h : tap_h + height, tap_w : tap_w + across, :]
                total = total + jnp.einsum(
                    "fhwc,cd->fhwd",
                    window,
                    piece[:, tap_t, tap_h, tap_w, :],
                    preferred_element_type=jnp.float32,
                )
    summed = (inputs + total).astype(jnp.bfloat16)
    normed = normalize(summed.astype(jnp.float32), attn_gain).astype(jnp.bfloat16)
    flat = normed.reshape(depth, height * across, width)
    positions = height * across
    initial = (
        jnp.full((depth, positions), -1e30, jnp.float32),
        jnp.zeros((depth, positions), jnp.float32),
        jnp.zeros((depth, positions, width), jnp.float32),
    )
    projected = jnp.einsum("fpc,cd->fpd", flat, w_qkv, preferred_element_type=jnp.float32)
    queries = projected[:, :, :width].astype(jnp.bfloat16)
    keys = projected[:, :, width : 2 * width].astype(jnp.bfloat16)
    values = projected[:, :, 2 * width :].astype(jnp.bfloat16)
    result = absorb(
        initial,
        queries,
        lax.all_gather(keys, "rows", axis=1, tiled=True),
        lax.all_gather(values, "rows", axis=1, tiled=True),
    )
    mixed = (result[2] / result[1][:, :, None]).astype(jnp.bfloat16)
    attended = jnp.einsum("fpc,cd->fpd", mixed, w_out, preferred_element_type=jnp.float32).astype(
        jnp.bfloat16
    )
    return (summed, attended.reshape(depth, height, across, width))


def solution(mesh):
    return jax.shard_map(
        body,
        mesh=mesh,
        in_specs=(
            P(("groups", "tm"), "rows", None, None),
            P("groups"),
            P(),
            P("tm", None, None, None, None),
            P(),
            P(),
            P(),
        ),
        out_specs=(
            P(("groups", "tm"), "rows", None, None),
            P(("groups", "tm"), "rows", None, None),
        ),
        check_vma=False,
    )
```

```python
import jax
import jax.numpy as jnp
from jax import lax
from jax.sharding import PartitionSpec as P

C = 384


EPSILON = 1e-06


def passed_along(value, axis, steps):
    count = lax.axis_size(axis)
    leading, last = (max(0, -steps), min(count, count - steps))
    return lax.ppermute(value, axis, [(source, source + steps) for source in range(leading, last)])


def with_halo(cells, sides, width):
    for axis, dim in sides:
        count = lax.axis_size(axis)
        ends = count - 1
        head = lax.slice_in_dim(cells, 0, width, axis=dim)
        tail = lax.slice_in_dim(cells, cells.shape[dim] - width, cells.shape[dim], axis=dim)
        cells = jnp.concatenate(
            [
                lax.ppermute(tail, axis, [(i, (i + 1) % count) for i in range(ends)]),
                cells,
                lax.ppermute(head, axis, [((i + 1) % count, i) for i in range(ends)]),
            ],
            axis=dim,
        )
    return cells


def normalize(values, gain):
    mean_square = jnp.mean(values * values, axis=-1, keepdims=True)
    return values * lax.rsqrt(mean_square + EPSILON) * gain


def absorb(carry, queries, keys, values):
    running_max, running_sum, running_acc = carry
    scores = jnp.einsum("fqc,fkc->fqk", queries, keys, preferred_element_type=jnp.float32) * C ** (
        -0.5
    )
    new_max = jnp.maximum(running_max, jnp.max(scores, axis=-1))
    expo = jnp.exp(scores - new_max[:, :, None])
    new_sum = jnp.sum(expo, axis=-1)
    update = jnp.einsum(
        "fqk,fkc->fqc", expo.astype(jnp.bfloat16), values, preferred_element_type=jnp.float32
    )
    return (new_max, new_sum, update)


def body(frames, segment_ids, norm_gain, conv_weight, attn_gain, w_qkv, w_out):
    depth, height, across, width = frames.shape
    inputs = frames.astype(jnp.float32)
    activated = jax.nn.silu(normalize(inputs, norm_gain)).astype(jnp.bfloat16)
    first = lax.axis_index("tm") * depth
    padded_ids = jnp.concatenate([jnp.full((2,), -1, jnp.int32), segment_ids])
    local_ids = lax.dynamic_slice_in_dim(padded_ids, first, depth + 2)
    own_ids = local_ids[2:]
    earlier = passed_along(activated, "tm", 1)
    extended = with_halo(jnp.concatenate([earlier, activated], 0), (("rows", 1),), 1)
    extended = jnp.pad(extended, ((0, 0), (0, 0), (1, 1), (0, 0)))
    masked = jnp.stack(
        [
            extended[tap_t : tap_t + depth]
            * (local_ids[tap_t : tap_t + depth] == own_ids).astype(jnp.bfloat16)[
                :, None, None, None
            ]
            for tap_t in range(3)
        ]
    )
    total = jnp.zeros((depth, height, across, width), jnp.float32)
    flat_weight = conv_weight.reshape(conv_weight.shape[0], 27 * width)
    piece = lax.all_gather(flat_weight, "tm", axis=0, tiled=True)
    for tap_t in range(3):
        for tap_h in range(3):
            for tap_w in range(3):
                window = masked[tap_t, :, tap_h : tap_h + height, tap_w : tap_w + across, :]
                total = total + jnp.einsum(
                    "fhwc,cd->fhwd",
                    window,
                    piece[:, ((tap_t * 3 + tap_h) * 3 + tap_w) * width : ((tap_t * 3 + tap_h) * 3 + tap_w + 1) * width],
                    preferred_element_type=jnp.float32,
                )
    summed = (inputs + total).astype(jnp.bfloat16)
    normed = normalize(summed.astype(jnp.float32), attn_gain).astype(jnp.bfloat16)
    flat = normed.reshape(depth, height * across, width)
    positions = height * across
    initial = (
        jnp.full((depth, positions), -1e30, jnp.float32),
        jnp.zeros((depth, positions), jnp.float32),
        jnp.zeros((depth, positions, width), jnp.float32),
    )
    projected = jnp.einsum("fpc,cd->fpd", flat, w_qkv, preferred_element_type=jnp.float32)
    queries = projected[:, :, :width].astype(jnp.bfloat16)
    keys = projected[:, :, width : 2 * width].astype(jnp.bfloat16)
    values = projected[:, :, 2 * width :].astype(jnp.bfloat16)
    result = absorb(
        initial,
        queries,
        lax.all_gather(keys, "rows", axis=1, tiled=True),
        lax.all_gather(values, "rows", axis=1, tiled=True),
    )
    mixed = (result[2] / result[1][:, :, None]).astype(jnp.bfloat16)
    attended = jnp.einsum("fpc,cd->fpd", mixed, w_out, preferred_element_type=jnp.float32).astype(
        jnp.bfloat16
    )
    return (summed, attended.reshape(depth, height, across, width))


def solution(mesh):
    return jax.shard_map(
        body,
        mesh=mesh,
        in_specs=(
            P(("groups", "tm"), "rows", None, None),
            P("groups"),
            P(),
            P("tm", None, None, None, None),
            P(),
            P(),
            P(),
        ),
        out_specs=(
            P(("groups", "tm"), "rows", None, None),
            P(("groups", "tm"), "rows", None, None),
        ),
        check_vma=False,
    )
```

```python
import jax
import jax.numpy as jnp
from jax import lax
from jax.sharding import PartitionSpec as P

C = 384


EPSILON = 1e-06


def passed_along(value, axis, steps):
    count = lax.axis_size(axis)
    leading, last = (max(0, -steps), min(count, count - steps))
    return lax.ppermute(value, axis, [(source, source + steps) for source in range(leading, last)])


def with_halo(cells, sides, width):
    for axis, dim in sides:
        count = lax.axis_size(axis)
        ends = count - 1
        head = lax.slice_in_dim(cells, 0, width, axis=dim)
        tail = lax.slice_in_dim(cells, cells.shape[dim] - width, cells.shape[dim], axis=dim)
        cells = jnp.concatenate(
            [
                lax.ppermute(tail, axis, [(i, (i + 1) % count) for i in range(ends)]),
                cells,
                lax.ppermute(head, axis, [((i + 1) % count, i) for i in range(ends)]),
            ],
            axis=dim,
        )
    return cells


def normalize(values, gain):
    mean_square = jnp.mean(values * values, axis=-1, keepdims=True)
    return values * lax.rsqrt(mean_square + EPSILON) * gain


def absorb(carry, queries, keys, values):
    running_max, running_sum, running_acc = carry
    scores = jnp.einsum("fqc,fkc->fqk", queries, keys, preferred_element_type=jnp.float32) * C ** (
        -0.5
    )
    new_max = jnp.maximum(running_max, jnp.max(scores, axis=-1))
    expo = jnp.exp(scores - new_max[:, :, None])
    new_sum = jnp.sum(expo, axis=-1)
    update = jnp.einsum(
        "fqk,fkc->fqc", expo.astype(jnp.bfloat16), values, preferred_element_type=jnp.float32
    )
    return (new_max, new_sum, update)


def body(frames, segment_ids, norm_gain, conv_weight, attn_gain, w_qkv, w_out):
    depth, height, across, width = frames.shape
    inputs = frames.astype(jnp.float32)
    activated = jax.nn.silu(normalize(inputs, norm_gain)).astype(jnp.bfloat16)
    first = lax.axis_index("tm") * depth
    padded_ids = jnp.concatenate([jnp.full((2,), -1, jnp.int32), segment_ids])
    local_ids = lax.dynamic_slice_in_dim(padded_ids, first, depth + 2)
    own_ids = local_ids[2:]
    earlier = passed_along(activated, "tm", 1)
    extended = with_halo(jnp.concatenate([earlier, activated], 0), (("rows", 1),), 1)
    extended = jnp.pad(extended, ((0, 0), (0, 0), (1, 1), (0, 0)))
    masked = jnp.stack(
        [
            extended[tap_t : tap_t + depth]
            * (local_ids[tap_t : tap_t + depth] == own_ids).astype(jnp.bfloat16)[
                :, None, None, None
            ]
            for tap_t in range(3)
        ]
    )
    piece = lax.all_gather(conv_weight, "tm", axis=0, tiled=True)
    windows = jnp.stack(
        [
            masked[tap_t, :, tap_h : tap_h + height, tap_w : tap_w + across, :]
            for tap_t in range(3)
            for tap_h in range(3)
            for tap_w in range(3)
        ],
        axis=3,
    )
    total = jnp.einsum(
        "fhwtc,ctd->fhwd",
        windows,
        piece.reshape(width, 27, width),
        preferred_element_type=jnp.float32,
    )
    summed = (inputs + total).astype(jnp.bfloat16)
    normed = normalize(summed.astype(jnp.float32), attn_gain).astype(jnp.bfloat16)
    flat = normed.reshape(depth, height * across, width)
    positions = height * across
    initial = (
        jnp.full((depth, positions), -1e30, jnp.float32),
        jnp.zeros((depth, positions), jnp.float32),
        jnp.zeros((depth, positions, width), jnp.float32),
    )
    projected = jnp.einsum("fpc,cd->fpd", flat, w_qkv, preferred_element_type=jnp.float32)
    queries = projected[:, :, :width].astype(jnp.bfloat16)
    keys = projected[:, :, width : 2 * width].astype(jnp.bfloat16)
    values = projected[:, :, 2 * width :].astype(jnp.bfloat16)
    result = absorb(
        initial,
        queries,
        lax.all_gather(keys, "rows", axis=1, tiled=True),
        lax.all_gather(values, "rows", axis=1, tiled=True),
    )
    mixed = (result[2] / result[1][:, :, None]).astype(jnp.bfloat16)
    attended = jnp.einsum("fpc,cd->fpd", mixed, w_out, preferred_element_type=jnp.float32).astype(
        jnp.bfloat16
    )
    return (summed, attended.reshape(depth, height, across, width))


def solution(mesh):
    return jax.shard_map(
        body,
        mesh=mesh,
        in_specs=(
            P(("groups", "tm"), "rows", None, None),
            P("groups"),
            P(),
            P("tm", None, None, None, None),
            P(),
            P(),
            P(),
        ),
        out_specs=(
            P(("groups", "tm"), "rows", None, None),
            P(("groups", "tm"), "rows", None, None),
        ),
        check_vma=False,
    )
```
